512 devices in a mesh: rows: 64 (over y, x, core), grp: 8 (over z).
Axes of the slice: x: 4, y: 8, z: 8, core: 2. Of those that a mesh axis runs over, the one named last changes fastest.
Arguments:
- features: bfloat16 [524288, 256], P(('rows', 'grp')), may hold values from -1 to 1
- targets: bfloat16 [524288, 2048], P(('rows', 'grp')), may hold values from -6 to 6
- ridge: float32 [256], replicated, may hold values from 0.5 to 4
Outputs:
- readout: float32 [2048, 256], P('rows')
- factor: float32 [256, 256], replicated
The draws below stay inside these ranges and needn't reach their ends.
All inputs are finite; a program needn't handle non-finite values.
Results may differ from the reference program's by a relative error of at most 0.0003.
Values sent between devices are 32-bit elements; how exact they have to be, the bound alone decides.
A program may use at most 64 MiB of HBM per device.

```python
import math
import jax
import jax.numpy as jnp
from jax import lax

F = 256
C = 2048
ROW_DEV = 1024
ROWS_ALL = 524288


def draw_features(key, part):
    keys = jax.random.split(key, 4)
    scales = jnp.exp(jax.random.uniform(keys[0], (F,), jnp.float32, 0.0, math.log(8.0)))
    noise = jax.random.normal(keys[1], (ROWS_ALL, F), jnp.float32)
    common = jax.random.normal(keys[2], (ROWS_ALL, 1), jnp.float32)
    mixing = jax.random.uniform(keys[3], (F,), jnp.float32, -0.4, 0.4)
    values = (noise + common * mixing) * scales / math.sqrt(ROWS_ALL)
    return jnp.clip(values, -1.0, 1.0).astype(jnp.bfloat16)


def steps_of(key, extent, cuts, smallest, high):
    def one(axis_at, parts):
        draws = jax.random.uniform(jax.random.fold_in(jax.random.fold_in(key, 6), axis_at), (parts,), jnp.float32, smallest / len(cuts), high / len(cuts))
        return jnp.repeat(jnp.exp(draws), extent[axis_at] // parts).reshape((-1,) + (1,) * (len(extent) - axis_at - 1))

    level = one(*cuts[0])
    for cut in cuts[1:]:
        level = level * one(*cut)
    return level


def scatter_about(rng, shape, scale, most, shards=(), dtype=jnp.bfloat16):
    loudness = steps_of(rng, shape, shards, -0.22, 0.18) if shards else 1.0
    drawn = jax.random.normal(rng, shape, jnp.float32) * scale * loudness
    return jnp.minimum(jnp.maximum(drawn, -most), most).astype(dtype)


def setup_inputs(seed: int = 0) -> dict:
    streams_of = jax.random.split(jax.random.key(seed), 4)
    features = draw_features(jax.random.fold_in(streams_of[3], 71), 0)
    targets = scatter_about(streams_of[1], (ROWS_ALL, C), 1.0, 6.0, ((0, 512),))
    ridge = jnp.clip(jnp.exp(jax.random.uniform(streams_of[2], (F,), jnp.float32, math.log(0.5), math.log(4.0))), 0.5, 4.0)
    return dict(features=features, targets=targets, ridge=ridge)


def reference(features, targets, ridge):
    feat_blocks = features.reshape(-1, ROW_DEV, F)
    targ_blocks = targets.reshape(-1, ROW_DEV, C)
    dims = (((0,), (0,)), ((), ()))

    def accumulate(carry, pair):
        gram_sum, cross_sum = carry
        feat_rows, targ_rows = pair
        gram_sum = gram_sum + lax.dot_general(feat_rows.astype(jnp.float32), feat_rows.astype(jnp.float32), dims, preferred_element_type=jnp.float32)
        cross_sum = cross_sum + lax.dot_general(targ_rows.astype(jnp.float32), feat_rows.astype(jnp.float32), dims, preferred_element_type=jnp.float32)
        return ((gram_sum, cross_sum), None)
    start = (jnp.zeros((F, F), jnp.float32), jnp.zeros((C, F), jnp.float32))
    (gram_total, cross_total), _ = lax.scan(accumulate, start, (feat_blocks, targ_blocks))
    factor = jnp.linalg.cholesky(gram_total + jnp.diag(ridge)).T
    halfway = jax.scipy.linalg.solve_triangular(factor, cross_total.T, trans='T', lower=False)
    readout = jax.scipy.linalg.solve_triangular(factor, halfway, lower=False).T
    return (readout, factor)
```

```python
import functools
import jax, jax.numpy as jnp
from jax import lax
from jax.experimental import pallas as pl
from jax.experimental.pallas import tpu as pltpu
from jax.sharding import PartitionSpec as P

HI = lax.Precision.HIGHEST


def mm(a, b, ca=1, cb=0):
    return lax.dot_general(a, b, (((ca,), (cb,)), ((), ())), precision=HI, preferred_element_type=jnp.float32)

def rows8(v, i):
    return jnp.broadcast_to(v[i:i+1, :], (8, 128))

def lane(v, j):
    return jnp.broadcast_to(v[:, j:j+1], (8, 128))

def chol_block(a, u_ref, v_ref):
    lanes = lax.broadcasted_iota(jnp.int32, (8, 128), 1)
    subs = lax.broadcasted_iota(jnp.int32, (8, 128), 0)
    a = list(a)
    e = [jnp.where(lanes == subs + 8 * g, 1.0, 0.0).astype(jnp.float32) for g in range(16)]
    for s in range(16):
        k = 8 * s
        cols = [[lane(a[g], k + j) for j in range(8)] for g in range(s, 16)]
        low = [[rows8(cols[0][j], i) for j in range(i + 1)] for i in range(8)]
        arow = [rows8(a[s], j) for j in range(8)]
        erow = [rows8(e[s], j) for j in range(8)]
        for j in range(8):
            r = lax.rsqrt(low[j][j])
            arow[j] = arow[j] * r
            erow[j] = erow[j] * r
            for i in range(j + 1, 8):
                low[i][j] = low[i][j] * r
            for g in range(1, 16 - s):
                cols[g][j] = cols[g][j] * r
            for i in range(j + 1, 8):
                l = low[i][j]
                for m in range(j + 1, i + 1):
                    low[i][m] = low[i][m] - l * low[m][j]
                arow[i] = arow[i] - l * arow[j]
                erow[i] = erow[i] - l * erow[j]
                for g in range(1, 16 - s):
                    cols[g][i] = cols[g][i] - l * cols[g][j]
            for g in range(1, 16 - s):
                a[s + g] = a[s + g] - cols[g][j] * arow[j]
                e[s + g] = e[s + g] - cols[g][j] * erow[j]
        uo, vo = arow[0], erow[0]
        for j in range(1, 8):
            uo = jnp.where(subs == j, arow[j], uo)
            vo = jnp.where(subs == j, erow[j], vo)
        u_ref[pl.ds(k, 8), :] = jnp.where(lanes >= subs + k, uo, 0.0)
        v_ref[pl.ds(k, 8), :] = jnp.where(lanes <= subs + k, vo, 0.0)

def chol_kernel(g_ref, ridge_ref, c_ref, out_ref, fac_ref, u1, v1, u2, v2, s22):
    lanes = lax.broadcasted_iota(jnp.int32, (8, 128), 1)
    subs = lax.broadcasted_iota(jnp.int32, (8, 128), 0)
    def ridged(g, half):
        rr = jnp.broadcast_to(ridge_ref[0:1, half * 128:half * 128 + 128], (8, 128))
        return lambda tile: tile + jnp.where(lanes == subs + 8 * g, rr, 0.0)
    a11 = [ridged(g, 0)(g_ref[g]) for g in range(16)]
    chol_block(a11, u1, v1)
    a12 = g_ref[16:32].reshape(128, 128)
    u12 = mm(v1[...], a12)
    s22[...] = mm(u12, u12, 0, 0)
    a22 = [ridged(g, 1)(g_ref[32 + g]) - s22[pl.ds(8 * g, 8), :] for g in range(16)]
    chol_block(a22, u2, v2)
    c1 = jnp.concatenate([c_ref[2 * t] for t in range(4)], axis=0)
    c2 = jnp.concatenate([c_ref[2 * t + 1] for t in range(4)], axis=0)
    x1 = mm(c1, v1[...], 1, 1)
    x2 = mm(c2 - mm(x1, u12), v2[...], 1, 1)
    y2 = mm(x2, v2[...])
    y1 = mm(x1 - mm(y2, u12, 1, 1), v1[...])
    out_ref[:, 0:128] = y1
    out_ref[:, 128:256] = y2
    fac_ref[0:128, 0:128] = u1[...]
    fac_ref[0:128, 128:256] = u12
    fac_ref[128:256, 0:128] = jnp.zeros((128, 128), jnp.float32)
    fac_ref[128:256, 128:256] = u2[...]

def chol_call(g, ridge, c):
    sq = pltpu.VMEM((128, 128), jnp.float32)
    vm = pl.BlockSpec(memory_space=pltpu.VMEM)
    return pl.pallas_call(chol_kernel,
        out_shape=(jax.ShapeDtypeStruct((32, 256), jnp.float32), jax.ShapeDtypeStruct((256, 256), jnp.float32)),
        in_specs=[vm, vm, vm], out_specs=(vm, vm),
        scratch_shapes=[sq] * 5)(g, ridge, c)

MESH = pl.DeviceIdType.MESH
LANES = 128


class Place:
    def __init__(self, n, nx):
        self.n, self.nx = n, nx
        rows, self.z = lax.axis_index("rows"), lax.axis_index("grp")
        self.c = rows % 2
        self.x = (rows // 2) % nx
        self.y = rows // (2 * nx)
        self.a = self.y + self.c * (self.z - self.y)
        self.b = self.z + self.c * (self.y - self.z)

    def device(self, y, x, c, z):
        return ((y * self.nx + x) * 2 + c, z)

    def partner(self):
        return self.device(self.y, self.x, 1 - self.c, self.z)

    def on_a(self, p):
        return self.device(p + self.c * (self.y - p), self.x, self.c, self.z + self.c * (p - self.z))

    def on_b(self, p):
        return self.device(self.y + self.c * (p - self.y), self.x, self.c, p + self.c * (self.z - p))

    def on_x(self, p):
        return self.device(self.y, p, self.c, self.z)

    def on_z(self, p):
        return self.device(self.y, self.x, self.c, p)


def far_first(n):
    return sorted(range(1, n), key=lambda d: -min(d, n - d))


def near_first(n):
    return sorted(range(1, n), key=lambda d: min(d, n - d))


def comm_kernel(
    n, nx, cross_ref, g_ref, gout, cout,
    rc, rg, hg, g1, g2, g3, h, b1, s1, b2, s2, b3,
    pair_send, pair_recv, gs1, gr1, gs2, gr2, gs3, gr3, gs4, gr4, gs5, gr5,
    cs1, cr1, cs2, cr2, cs3, cr3, cs4, cr4,
):
    me = Place(n, nx)
    c = me.c
    gt, tz, half = 24 // n, 8 // n, 24
    sends = []

    def send(src, dst, ssem, rsem, device):
        copy = pltpu.make_async_remote_copy(
            src_ref=src, dst_ref=dst, send_sem=ssem, recv_sem=rsem, device_id=device, device_id_type=MESH
        )
        copy.start()
        sends.append(copy)

    def arrived(dst, rsem):
        pltpu.make_async_copy(dst, dst, rsem).wait()

    barrier = pltpu.get_barrier_semaphore()
    greet = [me.partner()]
    greet += [me.on_a((me.a + d) % n) for d in range(1, n)]
    greet += [me.on_b((me.b + d) % n) for d in range(1, n)]
    greet += [me.on_x((me.x + d) % nx) for d in range(1, nx)]
    for device in greet:
        pl.semaphore_signal(barrier, inc=1, device_id=device, device_id_type=MESH)
    pl.semaphore_wait(barrier, len(greet))

    send(g_ref.at[pl.ds((1 - c) * half, half)], rg, pair_send.at[0], pair_recv.at[0], me.partner())
    send(cross_ref.at[:, 1 - c], rc, pair_send.at[1], pair_recv.at[1], me.partner())

    arrived(rg, pair_recv.at[0])
    for p in range(n):
        hg[p] = g_ref[pl.ds(c * half + p * gt, gt)] + rg[pl.ds(p * gt, gt)]
    for d in far_first(n):
        p = (me.a + d) % n
        send(hg.at[p], g1.at[me.a], gs1.at[d], gr1.at[me.a], me.on_a(p))
    g1[me.a] = hg[me.a]

    arrived(rc, pair_recv.at[1])

    def fill(blk, carry):
        y, x = blk // nx, blk % nx
        for q in range(8):
            rt, lh = q // 2, q % 2
            z, t = q // tz, q % tz
            at = (pl.ds(8 * rt, 8), pl.ds(LANES * lh, LANES))
            h[y + c * (z - y), x, z + c * (y - z), t] = cross_ref[(blk, c) + at] + rc[(blk,) + at]
        return carry

    lax.fori_loop(0, n * nx, fill, 0)
    for d in far_first(n):
        p = (me.a + d) % n
        send(h.at[p], b1.at[me.a], cs1.at[d], cr1.at[me.a], me.on_a(p))

    for d in near_first(n):
        p = (me.a + d) % n
        arrived(g1.at[p], gr1.at[p])
    g2[me.x] = sum_slots(g1, n)
    for d in far_first(nx):
        send(g2.at[me.x], g2.at[me.x], gs2.at[d], gr2.at[me.x], me.on_x((me.x + d) % nx))
    for d in near_first(nx):
        p = (me.x + d) % nx
        arrived(g2.at[p], gr2.at[p])
    g3[me.b] = sum_slots(g2, nx)
    for d in far_first(n):
        send(g3.at[me.b], g3.at[me.b], gs3.at[d], gr3.at[me.b], me.on_b((me.b + d) % n))
    for d in near_first(n):
        p = (me.b + d) % n
        arrived(g3.at[p], gr3.at[p])

    def owned(p):
        return pl.ds(c * half + p * gt, gt)

    gout[owned(me.a)] = sum_slots(g3, n)
    for d in far_first(n):
        send(gout.at[owned(me.a)], gout.at[owned(me.a)], gs4.at[d], gr4.at[me.a], me.on_a((me.a + d) % n))
    send(gout.at[owned(me.a)], gout.at[owned(me.a)], gs5.at[me.a], gr5.at[me.a], me.partner())
    for d in near_first(n):
        p = (me.a + d) % n
        arrived(gout.at[owned(p)], gr4.at[p])
        send(gout.at[owned(p)], gout.at[owned(p)], gs5.at[p], gr5.at[p], me.partner())

    for d in near_first(n):
        p = (me.a + d) % n
        arrived(b1.at[p], cr1.at[p])

    def add1(x, carry):
        total = h[me.a, x]
        for d in range(1, n):
            total = total + b1[(me.a + d) % n, x]
        s1[x] = total
        return carry

    lax.fori_loop(0, nx, add1, 0)
    for d in far_first(nx):
        p = (me.x + d) % nx
        send(s1.at[p], b2.at[me.x], cs2.at[d], cr2.at[me.x], me.on_x(p))
    for d in near_first(nx):
        p = (me.x + d) % nx
        arrived(b2.at[p], cr2.at[p])
    total = s1[me.x]
    for d in range(1, nx):
        total = total + b2[(me.x + d) % nx]
    s2[...] = total
    for d in far_first(n):
        p = (me.b + d) % n
        send(s2.at[p], b3.at[me.b], cs3.at[d], cr3.at[me.b], me.on_b(p))
    for d in near_first(n):
        p = (me.b + d) % n
        arrived(b3.at[p], cr3.at[p])
    total = s2[me.b]
    for d in range(1, n):
        total = total + b3[(me.b + d) % n]
    mine = pl.ds(me.z * tz, tz)
    cout[mine] = total
    for d in far_first(n):
        send(cout.at[mine], cout.at[mine], cs4.at[d], cr4.at[me.z], me.on_z((me.z + d) % n))
    for p in range(n):
        pass
    for d in near_first(n):
        p = (me.z + d) % n
        arrived(cout.at[pl.ds(p * tz, tz)], cr4.at[p])
    for p in range(n):
        arrived(gout.at[pl.ds((1 - c) * half + p * gt, gt)], gr5.at[p])
    for copy in sends:
        copy.wait_send()


def sum_slots(ref, count):
    total = ref[0]
    for p in range(1, count):
        total = total + ref[p]
    return total


def comm_call(n, nx, cross, g):
    gt, tz = 24 // n, 8 // n
    f32 = lambda *lead: pltpu.VMEM(lead + (8, LANES), jnp.float32)
    dma = lambda k: pltpu.SemaphoreType.DMA((k,))
    vmem = pl.BlockSpec(memory_space=pltpu.VMEM)
    return pl.pallas_call(
        functools.partial(comm_kernel, n, nx),
        out_shape=(
            jax.ShapeDtypeStruct((48, 8, LANES), jnp.float32),
            jax.ShapeDtypeStruct((8, 8, LANES), jnp.float32),
        ),
        in_specs=[vmem, vmem],
        out_specs=(vmem, vmem),
        scratch_shapes=[
            pltpu.VMEM((n * nx, 32, 256), jnp.float32), f32(24), f32(n, gt), f32(n, gt), f32(nx, gt), f32(n, gt),
            f32(n, nx, n, tz), f32(n, nx, n, tz), f32(nx, n, tz), f32(nx, n, tz), f32(n, tz), f32(n, tz),
            dma(2), dma(2), dma(n), dma(n), dma(nx), dma(nx), dma(n), dma(n), dma(n), dma(n), dma(n), dma(n),
            dma(n), dma(n), dma(nx), dma(nx), dma(n), dma(n), dma(n), dma(n),
        ],
        compiler_params=pltpu.CompilerParams(collective_id=0, has_side_effects=True),
    )(cross, g)


def shards(n, nx, features, targets, ridge):
    dims = (((0,), (0,)), ((), ()))
    gram = lax.dot_general(features, features, dims, preferred_element_type=jnp.float32)
    cross = lax.dot_general(targets, features, dims, preferred_element_type=jnp.float32)
    tiles = jnp.concatenate([gram[:128, :128], gram[:128, 128:], gram[128:, 128:]], axis=0).reshape(48, 8, LANES)
    g, c = comm_call(n, nx, cross.reshape(n * nx, 2, 32, 256), tiles)
    return chol_call(g, ridge.reshape(1, 256), c)


def solution(mesh):
    n = mesh.shape["grp"]
    nx = mesh.shape["rows"] // (2 * n)
    return jax.shard_map(
        functools.partial(shards, n, nx),
        mesh=mesh,
        in_specs=(P(("rows", "grp"), None), P(("rows", "grp"), None), P()),
        out_specs=(P("rows", None), P()),
        check_vma=False,
    )
```

```python
import functools
import jax, jax.numpy as jnp
from jax import lax
from jax.experimental import pallas as pl
from jax.experimental.pallas import tpu as pltpu
from jax.sharding import PartitionSpec as P

HI = lax.Precision.HIGHEST


def mm(a, b, ca=1, cb=0):
    return lax.dot_general(a, b, (((ca,), (cb,)), ((), ())), precision=HI, preferred_element_type=jnp.float32)

def rows8(v, i):
    return jnp.broadcast_to(v[i:i+1, :], (8, 128))

def lane(v, j):
    return jnp.broadcast_to(v[:, j:j+1], (8, 128))

def chol_block(a, u_ref, v_ref, base, hooks):
    lanes = lax.broadcasted_iota(jnp.int32, (8, 128), 1)
    subs = lax.broadcasted_iota(jnp.int32, (8, 128), 0)
    a = list(a)
    e = [jnp.where(lanes == subs + 8 * g, 1.0, 0.0).astype(jnp.float32) for g in range(16)]
    for s in range(16):
        k = 8 * s
        if s in hooks:
            hooks[s]()
        cols = [[lane(a[g], k + j) for j in range(8)] for g in range(s, 16)]
        low = [[rows8(cols[0][j], i) for j in range(i + 1)] for i in range(8)]
        arow = [rows8(a[s], j) for j in range(8)]
        erow = [rows8(e[s], j) for j in range(8)]
        for j in range(8):
            r = lax.rsqrt(low[j][j])
            arow[j] = arow[j] * r
            erow[j] = erow[j] * r
            for i in range(j + 1, 8):
                low[i][j] = low[i][j] * r
            for g in range(1, 16 - s):
                cols[g][j] = cols[g][j] * r
            for i in range(j + 1, 8):
                l = low[i][j]
                for m in range(j + 1, i + 1):
                    low[i][m] = low[i][m] - l * low[m][j]
                arow[i] = arow[i] - l * arow[j]
                erow[i] = erow[i] - l * erow[j]
                for g in range(1, 16 - s):
                    cols[g][i] = cols[g][i] - l * cols[g][j]
            for g in range(1, 16 - s):
                a[s + g] = a[s + g] - cols[g][j] * arow[j]
                e[s + g] = e[s + g] - cols[g][j] * erow[j]
        uo, vo = arow[0], erow[0]
        for j in range(1, 8):
            uo = jnp.where(subs == j, arow[j], uo)
            vo = jnp.where(subs == j, erow[j], vo)
        u_ref[pl.ds(base + k, 8), pl.ds(base, 128)] = jnp.where(lanes >= subs + k, uo, 0.0)
        v_ref[pl.ds(base + k, 8), pl.ds(base, 128)] = jnp.where(lanes <= subs + k, vo, 0.0)

MESH = pl.DeviceIdType.MESH
LANES = 128


class Place:
    def __init__(self, n, nx):
        self.n, self.nx = n, nx
        rows, self.z = lax.axis_index("rows"), lax.axis_index("grp")
        self.c = rows % 2
        self.x = (rows // 2) % nx
        self.y = rows // (2 * nx)
        self.a = self.y + self.c * (self.z - self.y)
        self.b = self.z + self.c * (self.y - self.z)

    def device(self, y, x, c, z):
        return ((y * self.nx + x) * 2 + c, z)

    def partner(self):
        return self.device(self.y, self.x, 1 - self.c, self.z)

    def on_a(self, p):
        return self.device(p + self.c * (self.y - p), self.x, self.c, self.z + self.c * (p - self.z))

    def on_b(self, p):
        return self.device(self.y + self.c * (p - self.y), self.x, self.c, p + self.c * (self.z - p))

    def on_x(self, p):
        return self.device(self.y, p, self.c, self.z)

    def on_z(self, p):
        return self.device(self.y, self.x, self.c, p)


def far_first(n):
    return sorted(range(1, n), key=lambda d: -min(d, n - d))


def near_first(n):
    return sorted(range(1, n), key=lambda d: min(d, n - d))


def sum_slots(ref, count):
    total = ref[0]
    for p in range(1, count):
        total = total + ref[p]
    return total


def ridge_kernel(
    n, nx, f_hbm, t_hbm, ridge_ref, out_ref, fac_ref,
    feat, targ, cross, gram, gsum, csum, v_ref, q_ref,
    rc, rg, hg, g1, g2, g3, h, b1, s1, b2, s2, b3,
    load, gpair_s, gpair_r, cpair_s, cpair_r,
    gs1, gr1, gs2, gr2, gs3, gr3, gs4, gr4, gs5, gr5,
    cs1, cr1, cs2, cr2, cs3, cr3, cs4, cr4,
):
    me = Place(n, nx)
    c = me.c
    gt, tz, half = 24 // n, 8 // n, 24
    width = nx * 64
    sends = []

    def remote(src, dst, ssem, rsem, device):
        return pltpu.make_async_remote_copy(
            src_ref=src, dst_ref=dst, send_sem=ssem, recv_sem=rsem, device_id=device, device_id_type=MESH
        )

    def send(*what):
        copy = remote(*what)
        copy.start()
        sends.append(copy)

    def arrived(dst, rsem):
        pltpu.make_async_copy(dst, dst, rsem).wait()

    def columns(y):
        return pl.ds(pl.multiple_of(y * width, width), width)

    def load_targets(y):
        return pltpu.make_async_copy(t_hbm.at[:, columns(y)], targ.at[y], load.at[y])

    load_features = pltpu.make_async_copy(f_hbm, feat, load.at[n])
    load_features.start()
    for y in range(n):
        load_targets(y).start()

    barrier = pltpu.get_barrier_semaphore()
    greet = [me.partner()]
    greet += [me.on_a((me.a + d) % n) for d in far_first(n)]
    greet += [me.on_b((me.b + d) % n) for d in far_first(n)]
    greet += [me.on_x((me.x + d) % nx) for d in far_first(nx)]
    for device in greet:
        pl.semaphore_signal(barrier, inc=1, device_id=device, device_id_type=MESH)

    over_rows = (((0,), (0,)), ((), ()))
    load_features.wait()
    whole = lax.dot_general(feat[...], feat[...], over_rows, preferred_element_type=jnp.float32)
    gram[0:16] = whole[0:128, 0:128].reshape(16, 8, LANES)
    gram[16:32] = whole[0:128, 128:256].reshape(16, 8, LANES)
    gram[32:48] = whole[128:256, 128:256].reshape(16, 8, LANES)
    pl.semaphore_wait(barrier, len(greet))
    send(gram.at[pl.ds((1 - c) * half, half)], rg, gpair_s, gpair_r, me.partner())

    def pair(y):
        at = pl.ds(y * nx, nx)
        return remote(cross.at[at, 1 - c], rc.at[at], cpair_s.at[y], cpair_r.at[y], me.partner())

    def multiply(y, carry):
        load_targets(y).wait()
        block = lax.dot_general(targ[y], feat[...], over_rows, preferred_element_type=jnp.float32)
        cross[pl.ds(y * nx, nx)] = block.reshape(nx, 2, 32, 256)
        pair(y).start()
        return carry

    lax.fori_loop(0, n // 2, multiply, 0)
    arrived(rg, gpair_r)
    for p in range(n):
        hg[p] = gram[pl.ds(c * half + p * gt, gt)] + rg[pl.ds(p * gt, gt)]
    for d in far_first(n):
        p = (me.a + d) % n
        send(hg.at[p], g1.at[me.a], gs1.at[d], gr1.at[me.a], me.on_a(p))
    g1[me.a] = hg[me.a]
    lax.fori_loop(n // 2, n, multiply, 0)

    def fill(y, carry):
        arrived(rc.at[pl.ds(y * nx, nx)], cpair_r.at[y])
        for x in range(nx):
            blk = y * nx + x
            for q in range(8):
                rt, lh = q // 2, q % 2
                z, t = q // tz, q % tz
                at = (pl.ds(8 * rt, 8), pl.ds(LANES * lh, LANES))
                h[y + c * (z - y), x, z + c * (y - z), t] = cross[(blk, c) + at] + rc[(blk,) + at]
        return carry

    lax.fori_loop(0, n, fill, 0)
    for d in far_first(n):
        p = (me.a + d) % n
        send(h.at[p], b1.at[me.a], cs1.at[d], cr1.at[me.a], me.on_a(p))

    for d in near_first(n):
        p = (me.a + d) % n
        arrived(g1.at[p], gr1.at[p])
    g2[me.x] = sum_slots(g1, n)
    for d in far_first(nx):
        send(g2.at[me.x], g2.at[me.x], gs2.at[d], gr2.at[me.x], me.on_x((me.x + d) % nx))
    for d in near_first(nx):
        p = (me.x + d) % nx
        arrived(g2.at[p], gr2.at[p])
    g3[me.b] = sum_slots(g2, nx)
    for d in far_first(n):
        send(g3.at[me.b], g3.at[me.b], gs3.at[d], gr3.at[me.b], me.on_b((me.b + d) % n))
    for d in near_first(n):
        p = (me.b + d) % n
        arrived(g3.at[p], gr3.at[p])

    def owned(p):
        return pl.ds(c * half + p * gt, gt)

    gsum[owned(me.a)] = sum_slots(g3, n)
    for d in far_first(n):
        send(gsum.at[owned(me.a)], gsum.at[owned(me.a)], gs4.at[d], gr4.at[me.a], me.on_a((me.a + d) % n))
    send(gsum.at[owned(me.a)], gsum.at[owned(me.a)], gs5.at[me.a], gr5.at[me.a], me.partner())
    for d in near_first(n):
        p = (me.a + d) % n
        arrived(gsum.at[owned(p)], gr4.at[p])
        send(gsum.at[owned(p)], gsum.at[owned(p)], gs5.at[p], gr5.at[p], me.partner())
    for p in range(n):
        arrived(gsum.at[pl.ds((1 - c) * half + p * gt, gt)], gr5.at[p])

    def sum_a():
        for d in near_first(n):
            p = (me.a + d) % n
            arrived(b1.at[p], cr1.at[p])

        def add(x, carry):
            total = h[me.a, x]
            for d in range(1, n):
                total = total + b1[(me.a + d) % n, x]
            s1[x] = total
            return carry

        lax.fori_loop(0, nx, add, 0)
        for d in far_first(nx):
            p = (me.x + d) % nx
            send(s1.at[p], b2.at[me.x], cs2.at[d], cr2.at[me.x], me.on_x(p))

    def sum_x():
        total = s1[me.x]
        for d in near_first(nx):
            p = (me.x + d) % nx
            arrived(b2.at[p], cr2.at[p])
            total = total + b2[p]
        s2[...] = total
        for d in far_first(n):
            p = (me.b + d) % n
            send(s2.at[p], b3.at[me.b], cs3.at[d], cr3.at[me.b], me.on_b(p))

    mine = pl.ds(me.z * tz, tz)

    def sum_b():
        total = s2[me.b]
        for d in near_first(n):
            p = (me.b + d) % n
            arrived(b3.at[p], cr3.at[p])
            total = total + b3[p]
        csum[mine] = total
        for d in far_first(n):
            send(csum.at[mine], csum.at[mine], cs4.at[d], cr4.at[me.z], me.on_z((me.z + d) % n))

    lanes = lax.broadcasted_iota(jnp.int32, (8, 128), 1)
    subs = lax.broadcasted_iota(jnp.int32, (8, 128), 0)

    def ridged(tile, g, start):
        values = jnp.broadcast_to(ridge_ref[0:1, start:start + 128], (8, 128))
        return tile + jnp.where(lanes == subs + 8 * g, values, 0.0)

    chol_block([ridged(gsum[g], g, 0) for g in range(16)], fac_ref, v_ref, 0, first_hooks(sum_a, sum_x, sum_b))
    v11 = v_ref[0:128, 0:128]
    u12 = mm(v11, gsum[16:32].reshape(128, 128))
    fac_ref[0:128, 128:256] = u12
    fac_ref[128:256, 0:128] = jnp.zeros((128, 128), jnp.float32)
    v_ref[0:128, 128:256] = jnp.zeros((128, 128), jnp.float32)
    q_ref[0] = mm(u12, u12, 0, 0)
    q_ref[1] = mm(u12, v11, 0, 0)
    trailing = [ridged(gsum[32 + g], g, 128) - q_ref[0, pl.ds(8 * g, 8), :] for g in range(16)]
    chol_block(trailing, fac_ref, v_ref, 128, second_hooks(sum_a, sum_x, sum_b))
    v_ref[128:256, 0:128] = -mm(v_ref[128:256, 128:256], q_ref[1])

    for d in near_first(n):
        p = (me.z + d) % n
        arrived(csum.at[pl.ds(p * tz, tz)], cr4.at[p])
    left = jnp.concatenate([csum[2 * t] for t in range(4)], axis=0)
    right = jnp.concatenate([csum[2 * t + 1] for t in range(4)], axis=0)
    halfway = mm(jnp.concatenate([left, right], axis=1), v_ref[...], 1, 1)
    out_ref[...] = mm(halfway, v_ref[...])

    def sent(y, carry):
        pair(y).wait_send()
        return carry

    lax.fori_loop(0, n, sent, 0)
    for copy in sends:
        copy.wait_send()


def first_hooks(sum_a, sum_x, sum_b):
    return {2: sum_a, 13: sum_x}


def second_hooks(sum_a, sum_x, sum_b):
    return {6: sum_b}


def ridge_call(n, nx, features, targets, ridge):
    gt, tz = 24 // n, 8 // n
    rows = features.shape[0]
    f32 = lambda *shape: pltpu.VMEM(shape, jnp.float32)
    tiles = lambda *lead: f32(*lead, 8, LANES)
    dma = lambda k: pltpu.SemaphoreType.DMA((k,))
    one = pltpu.SemaphoreType.DMA
    vmem, hbm = pl.BlockSpec(memory_space=pltpu.VMEM), pl.BlockSpec(memory_space=pltpu.HBM)
    return pl.pallas_call(
        functools.partial(ridge_kernel, n, nx),
        out_shape=(
            jax.ShapeDtypeStruct((32, 256), jnp.float32),
            jax.ShapeDtypeStruct((256, 256), jnp.float32),
        ),
        in_specs=[hbm, hbm, vmem],
        out_specs=(vmem, vmem),
        scratch_shapes=[
            pltpu.VMEM((rows, 256), jnp.bfloat16), pltpu.VMEM((n, rows, nx * 64), jnp.bfloat16),
            f32(n * nx, 2, 32, 256), tiles(48), tiles(48), tiles(8), f32(256, 256), f32(2, 128, 128),
            f32(n * nx, 32, 256), tiles(24), tiles(n, gt), tiles(n, gt), tiles(nx, gt), tiles(n, gt),
            tiles(n, nx, n, tz), tiles(n, nx, n, tz), tiles(nx, n, tz), tiles(nx, n, tz), tiles(n, tz), tiles(n, tz),
            dma(n + 1), one, one, dma(n), dma(n),
            dma(n), dma(n), dma(nx), dma(nx), dma(n), dma(n), dma(n), dma(n), dma(n), dma(n),
            dma(n), dma(n), dma(nx), dma(nx), dma(n), dma(n), dma(n), dma(n),
        ],
        compiler_params=pltpu.CompilerParams(collective_id=0, has_side_effects=True),
    )(features, targets, ridge)


def shards(n, nx, features, targets, ridge):
    return ridge_call(n, nx, features, targets, ridge.reshape(1, 256))


def solution(mesh):
    n = mesh.shape["grp"]
    nx = mesh.shape["rows"] // (2 * n)
    return jax.shard_map(
        functools.partial(shards, n, nx),
        mesh=mesh,
        in_specs=(P(("rows", "grp"), None), P(("rows", "grp"), None), P()),
        out_specs=(P("rows", None), P()),
        check_vma=False,
    )
```

```python
import functools
import jax, jax.numpy as jnp
from jax import lax
from jax.experimental import pallas as pl
from jax.experimental.pallas import tpu as pltpu
from jax.sharding import PartitionSpec as P

HI = lax.Precision.HIGHEST


def mm(a, b, ca=1, cb=0):
    return lax.dot_general(a, b, (((ca,), (cb,)), ((), ())), precision=HI, preferred_element_type=jnp.float32)

def rows8(v, i):
    return jnp.broadcast_to(v[i:i+1, :], (8, 128))

def gl(v, j):
    return jnp.take_along_axis(v, jnp.full((8, 128), j, jnp.int32), axis=1)

def chol_block(a, u_ref, v_ref, base, hooks):
    lanes = lax.broadcasted_iota(jnp.int32, (8, 128), 1)
    subs = lax.broadcasted_iota(jnp.int32, (8, 128), 0)
    m = list(a)

    def spread(s):
        arow = [rows8(m[s], j) for j in range(8)]
        low = [[gl(arow[j], 8 * s + i) for j in range(i + 1)] for i in range(8)]
        return arow, low

    ahead = spread(0)
    for s in range(16):
        k = 8 * s
        if s in hooks:
            hooks[s]()
        inside = (lanes >= k) & (lanes < k + 8)
        arow, low = ahead
        near = [gl(m[s + 1], k + j) for j in range(8)] if s < 15 else None
        mixed = jnp.where(inside, jnp.where(lanes == subs + k, 1.0, 0.0), m[s])
        mrow = [rows8(mixed, j) for j in range(8)]
        bycol = [[gl(m[g], k + j) for g in range(s + 2, 16)] for j in range(8)]
        far = list(zip(*bycol))
        if s < 15:
            nxt = jnp.where(inside, 0.0, m[s + 1])
        rs = []
        for j in range(8):
            r = lax.rsqrt(low[j][j])
            rs.append(r)
            for i in range(j + 1, 8):
                low[i][j] = low[i][j] * r
            for i in range(j + 1, 8):
                for t in range(j + 1, i + 1):
                    low[i][t] = low[i][t] - low[i][j] * low[t][j]
            mrow[j] = mrow[j] * r
            for i in range(j + 1, 8):
                mrow[i] = mrow[i] - low[i][j] * mrow[j]
            if s < 15:
                near[j] = near[j] * r
                for i in range(j + 1, 8):
                    near[i] = near[i] - low[i][j] * near[j]
                nxt = nxt - near[j] * mrow[j]
        if s < 15:
            m[s + 1] = nxt
            ahead = spread(s + 1)
        if far:
            w = list(mrow)
            for j in reversed(range(8)):
                w[j] = w[j] * rs[j]
                for i in range(j):
                    w[i] = w[i] - low[j][i] * w[j]
            for g, cols in enumerate(far, start=s + 2):
                out = jnp.where(inside, 0.0, m[g])
                for j in range(8):
                    out = out - cols[j] * w[j]
                m[g] = out
        for j in range(8):
            arow[j] = arow[j] * rs[j]
            for i in range(j + 1, 8):
                arow[i] = arow[i] - low[i][j] * arow[j]
        uo, vo = arow[0], mrow[0]
        for j in range(1, 8):
            uo = jnp.where(subs == j, arow[j], uo)
            vo = jnp.where(subs == j, mrow[j], vo)
        u_ref[pl.ds(base + k, 8), pl.ds(base, 128)] = jnp.where(lanes >= subs + k, uo, 0.0)
        v_ref[pl.ds(base + k, 8), pl.ds(base, 128)] = jnp.where(lanes <= subs + k, vo, 0.0)

MESH = pl.DeviceIdType.MESH
LANES = 128


class Place:
    def __init__(self, n, nx):
        self.n, self.nx = n, nx
        rows, self.z = lax.axis_index("rows"), lax.axis_index("grp")
        self.c = rows % 2
        self.x = (rows // 2) % nx
        self.y = rows // (2 * nx)
        self.a = self.y + self.c * (self.z - self.y)
        self.b = self.z + self.c * (self.y - self.z)

    def device(self, y, x, c, z):
        return ((y * self.nx + x) * 2 + c, z)

    def partner(self):
        return self.device(self.y, self.x, 1 - self.c, self.z)

    def on_a(self, p):
        return self.device(p + self.c * (self.y - p), self.x, self.c, self.z + self.c * (p - self.z))

    def on_b(self, p):
        return self.device(self.y + self.c * (p - self.y), self.x, self.c, p + self.c * (self.z - p))

    def on_x(self, p):
        return self.device(self.y, p, self.c, self.z)

    def on_z(self, p):
        return self.device(self.y, self.x, self.c, p)


def far_first(n):
    return sorted(range(1, n), key=lambda d: -min(d, n - d))


def near_first(n):
    return sorted(range(1, n), key=lambda d: min(d, n - d))


def sum_slots(ref, count):
    total = ref[0]
    for p in range(1, count):
        total = total + ref[p]
    return total


def ridge_kernel(
    n, nx, f_hbm, t_hbm, ridge_ref, out_ref, fac_ref,
    feat, targ, cross, gram, gsum, csum, v_ref, q_ref,
    rc, rg, hg, g1, g2, g3, hx, bx1, sx, bx2, ha, ba1, sa, ba2, s2, b3,
    load, gpair_s, gpair_r, cpair_s, cpair_r,
    gs1, gr1, gs2, gr2, gs3, gr3, gs4, gr4, gs5, gr5,
    xs1, xr1, xs2, xr2, as1, ar1, as2, ar2, cs3, cr3, cs4, cr4,
):
    me = Place(n, nx)
    c = me.c
    gt, tz, half = 24 // n, 8 // n, 24
    width = nx * 64
    sends = []

    def remote(src, dst, ssem, rsem, device):
        return pltpu.make_async_remote_copy(
            src_ref=src, dst_ref=dst, send_sem=ssem, recv_sem=rsem, device_id=device, device_id_type=MESH
        )

    def send(*what):
        copy = remote(*what)
        copy.start()
        sends.append(copy)

    def arrived(dst, rsem):
        pltpu.make_async_copy(dst, dst, rsem).wait()

    def columns(y):
        return pl.ds(pl.multiple_of(y * width, width), width)

    def load_targets(y):
        return pltpu.make_async_copy(t_hbm.at[:, columns(y)], targ.at[y], load.at[y])

    load_features = pltpu.make_async_copy(f_hbm, feat, load.at[n])
    load_features.start()
    for y in range(n):
        load_targets(y).start()

    barrier = pltpu.get_barrier_semaphore()
    greet = [me.partner()]
    greet += [me.on_a((me.a + d) % n) for d in far_first(n)]
    greet += [me.on_b((me.b + d) % n) for d in far_first(n)]
    greet += [me.on_x((me.x + d) % nx) for d in far_first(nx)]
    for device in greet:
        pl.semaphore_signal(barrier, inc=1, device_id=device, device_id_type=MESH)

    over_rows = (((0,), (0,)), ((), ()))
    load_features.wait()
    whole = lax.dot_general(feat[...], feat[...], over_rows, preferred_element_type=jnp.float32)
    gram[0:16] = whole[0:128, 0:128].reshape(16, 8, LANES)
    gram[16:32] = whole[0:128, 128:256].reshape(16, 8, LANES)
    gram[32:48] = whole[128:256, 128:256].reshape(16, 8, LANES)
    pl.semaphore_wait(barrier, len(greet))
    send(gram.at[pl.ds((1 - c) * half, half)], rg, gpair_s, gpair_r, me.partner())

    def pair(y):
        at = pl.ds(y * nx, nx)
        return remote(cross.at[at, 1 - c], rc.at[at], cpair_s.at[y], cpair_r.at[y], me.partner())

    def turn(i):
        return (me.y + n // 2 + i) % n

    def multiply(i, carry):
        y = turn(i)
        load_targets(y).wait()
        block = lax.dot_general(targ[y], feat[...], over_rows, preferred_element_type=jnp.float32)
        cross[pl.ds(y * nx, nx)] = block.reshape(nx, 2, 32, 256)
        pair(y).start()
        return carry

    def pass_on(i):
        y = turn(i)
        arrived(rc.at[pl.ds(y * nx, nx)], cpair_r.at[y])
        for x in range(nx):
            blk = y * nx + x
            for q in range(8):
                rt, lh = q // 2, q % 2
                z, t = q // tz, q % tz
                upper = (pl.ds(8 * rt, 4), pl.ds(LANES * lh, LANES))
                lower = (pl.ds(8 * rt + 4, 4), pl.ds(LANES * lh, LANES))
                hx[x, y, z, t] = cross[(blk, c) + upper] + rc[(blk,) + upper]
                ha[y + c * (z - y), z + c * (y - z), x, t] = cross[(blk, c) + lower] + rc[(blk,) + lower]
        for d in far_first(nx):
            p = (me.x + d) % nx
            remote(hx.at[p, y], bx1.at[me.x, y], xs1.at[p], xr1.at[me.x], me.on_x(p)).start()

        @pl.when((c == 0) & (y != me.y))
        def _():
            remote(ha.at[y], ba1.at[me.a], as1.at[y], ar1.at[me.a], me.on_a(y)).start()

        @pl.when(c == 1)
        def _():
            for d in far_first(n):
                p = (me.a + d) % n
                remote(ha.at[p, y], ba1.at[me.a, y], as1.at[p], ar1.at[me.a], me.on_a(p)).start()

    def both(i, carry):
        multiply(i, carry)
        pass_on(i - n // 2)
        return carry

    def rest(i, carry):
        pass_on(i)
        return carry

    lax.fori_loop(0, n // 2, multiply, 0)
    arrived(rg, gpair_r)
    for p in range(n):
        hg[p] = gram[pl.ds(c * half + p * gt, gt)] + rg[pl.ds(p * gt, gt)]
    for d in far_first(n):
        p = (me.a + d) % n
        send(hg.at[p], g1.at[me.a], gs1.at[d], gr1.at[me.a], me.on_a(p))
    g1[me.a] = hg[me.a]
    lax.fori_loop(n // 2, n, both, 0)
    lax.fori_loop(n // 2, n, rest, 0)

    def sum_first():
        for d in near_first(nx):
            p = (me.x + d) % nx
            arrived(bx1.at[p], xr1.at[p])

        def add_x(p, carry):
            for r in range(n):
                y, z = p + c * (r - p), r + c * (p - r)
                total = hx[me.x, y, z]
                for d in range(1, nx):
                    total = total + bx1[(me.x + d) % nx, y, z]
                sx[p, r] = total
            return carry

        lax.fori_loop(0, n, add_x, 0)
        for d in far_first(n):
            p = (me.a + d) % n
            send(sx.at[p], bx2.at[me.a], xs2.at[d], xr2.at[me.a], me.on_a(p))
        for d in near_first(n):
            p = (me.a + d) % n
            arrived(ba1.at[p], ar1.at[p])

        def add_a(r, carry):
            for x in range(nx):
                total = ha[me.a, r, x]
                for d in range(1, n):
                    total = total + ba1[(me.a + d) % n, r, x]
                sa[x, r] = total
            return carry

        lax.fori_loop(0, n, add_a, 0)
        for d in far_first(nx):
            p = (me.x + d) % nx
            send(sa.at[p], ba2.at[me.x], as2.at[d], ar2.at[me.x], me.on_x(p))

    def sum_second():
        total = sa[me.x]
        for d in near_first(nx):
            p = (me.x + d) % nx
            arrived(ba2.at[p], ar2.at[p])
            total = total + ba2[p]
        s2[:, :, 4:8, :] = total
        total = sx[me.a]
        for d in near_first(n):
            p = (me.a + d) % n
            arrived(bx2.at[p], xr2.at[p])
            total = total + bx2[p]
        s2[:, :, 0:4, :] = total
        for d in far_first(n):
            p = (me.b + d) % n
            send(s2.at[p], b3.at[me.b], cs3.at[d], cr3.at[me.b], me.on_b(p))

    mine = pl.ds(me.z * tz, tz)

    def sum_third():
        total = s2[me.b]
        for d in near_first(n):
            p = (me.b + d) % n
            arrived(b3.at[p], cr3.at[p])
            total = total + b3[p]
        csum[mine] = total
        for d in far_first(n):
            send(csum.at[mine], csum.at[mine], cs4.at[d], cr4.at[me.z], me.on_z((me.z + d) % n))

    for d in near_first(n):
        p = (me.a + d) % n
        arrived(g1.at[p], gr1.at[p])
    g2[me.x] = sum_slots(g1, n)
    for d in far_first(nx):
        send(g2.at[me.x], g2.at[me.x], gs2.at[d], gr2.at[me.x], me.on_x((me.x + d) % nx))
    for d in near_first(nx):
        p = (me.x + d) % nx
        arrived(g2.at[p], gr2.at[p])
    g3[me.b] = sum_slots(g2, nx)
    for d in far_first(n):
        send(g3.at[me.b], g3.at[me.b], gs3.at[d], gr3.at[me.b], me.on_b((me.b + d) % n))
    sum_first()
    for d in near_first(n):
        p = (me.b + d) % n
        arrived(g3.at[p], gr3.at[p])

    def owned(p):
        return pl.ds(c * half + p * gt, gt)

    gsum[owned(me.a)] = sum_slots(g3, n)
    for d in far_first(n):
        send(gsum.at[owned(me.a)], gsum.at[owned(me.a)], gs4.at[d], gr4.at[me.a], me.on_a((me.a + d) % n))
    send(gsum.at[owned(me.a)], gsum.at[owned(me.a)], gs5.at[me.a], gr5.at[me.a], me.partner())
    sum_second()
    for d in near_first(n):
        p = (me.a + d) % n
        arrived(gsum.at[owned(p)], gr4.at[p])
        send(gsum.at[owned(p)], gsum.at[owned(p)], gs5.at[p], gr5.at[p], me.partner())
    for p in range(n):
        arrived(gsum.at[pl.ds((1 - c) * half + p * gt, gt)], gr5.at[p])

    lanes = lax.broadcasted_iota(jnp.int32, (8, 128), 1)
    subs = lax.broadcasted_iota(jnp.int32, (8, 128), 0)

    def ridged(tile, g, start):
        values = jnp.broadcast_to(ridge_ref[0:1, start:start + 128], (8, 128))
        return tile + jnp.where(lanes == subs + 8 * g, values, 0.0)

    chol_block([ridged(gsum[g], g, 0) for g in range(16)], fac_ref, v_ref, 0, {4: sum_third})
    v11 = v_ref[0:128, 0:128]
    u12 = mm(v11, gsum[16:32].reshape(128, 128))
    fac_ref[0:128, 128:256] = u12
    fac_ref[128:256, 0:128] = jnp.zeros((128, 128), jnp.float32)
    v_ref[0:128, 128:256] = jnp.zeros((128, 128), jnp.float32)
    q_ref[0] = mm(u12, u12, 0, 0)
    q_ref[1] = mm(u12, v11, 0, 0)
    trailing = [ridged(gsum[32 + g], g, 128) - q_ref[0, pl.ds(8 * g, 8), :] for g in range(16)]
    chol_block(trailing, fac_ref, v_ref, 128, {})
    v_ref[128:256, 0:128] = -mm(v_ref[128:256, 128:256], q_ref[1])

    for d in near_first(n):
        p = (me.z + d) % n
        arrived(csum.at[pl.ds(p * tz, tz)], cr4.at[p])
    left = jnp.concatenate([csum[2 * t] for t in range(4)], axis=0)
    right = jnp.concatenate([csum[2 * t + 1] for t in range(4)], axis=0)
    halfway = mm(jnp.concatenate([left, right], axis=1), v_ref[...], 1, 1)
    out_ref[...] = mm(halfway, v_ref[...])

    def sent(y, carry):
        pair(y).wait_send()
        return carry

    lax.fori_loop(0, n, sent, 0)
    for d in range(1, nx):
        p = (me.x + d) % nx
        remote(hx.at[p], bx1.at[me.x], xs1.at[p], xr1.at[me.x], me.on_x(p)).wait_send()
    for d in range(1, n):
        p = (me.a + d) % n
        remote(ha.at[p], ba1.at[me.a], as1.at[p], ar1.at[me.a], me.on_a(p)).wait_send()
    for copy in sends:
        copy.wait_send()


def ridge_call(n, nx, features, targets, ridge):
    gt, tz = 24 // n, 8 // n
    rows = features.shape[0]
    f32 = lambda *shape: pltpu.VMEM(shape, jnp.float32)
    tiles = lambda *lead: f32(*lead, 8, LANES)
    halves = lambda *lead: f32(*lead, 4, LANES)
    dma = lambda k: pltpu.SemaphoreType.DMA((k,))
    one = pltpu.SemaphoreType.DMA
    vmem, hbm = pl.BlockSpec(memory_space=pltpu.VMEM), pl.BlockSpec(memory_space=pltpu.HBM)
    return pl.pallas_call(
        functools.partial(ridge_kernel, n, nx),
        out_shape=(
            jax.ShapeDtypeStruct((32, 256), jnp.float32),
            jax.ShapeDtypeStruct((256, 256), jnp.float32),
        ),
        in_specs=[hbm, hbm, vmem],
        out_specs=(vmem, vmem),
        scratch_shapes=[
            pltpu.VMEM((rows, 256), jnp.bfloat16), pltpu.VMEM((n, rows, nx * 64), jnp.bfloat16),
            f32(n * nx, 2, 32, 256), tiles(48), tiles(48), tiles(8), f32(256, 256), f32(2, 128, 128),
            f32(n * nx, 32, 256), tiles(24), tiles(n, gt), tiles(n, gt), tiles(nx, gt), tiles(n, gt),
            halves(nx, n, n, tz), halves(nx, n, n, tz), halves(n, n, tz), halves(n, n, tz),
            halves(n, n, nx, tz), halves(n, n, nx, tz), halves(nx, n, tz), halves(nx, n, tz), tiles(n, tz), tiles(n, tz),
            dma(n + 1), one, one, dma(n), dma(n),
            dma(n), dma(n), dma(nx), dma(nx), dma(n), dma(n), dma(n), dma(n), dma(n), dma(n),
            dma(nx), dma(nx), dma(n), dma(n), dma(n), dma(n), dma(nx), dma(nx), dma(n), dma(n), dma(n), dma(n),
        ],
        compiler_params=pltpu.CompilerParams(collective_id=0, has_side_effects=True),
    )(features, targets, ridge)


def shards(n, nx, features, targets, ridge):
    return ridge_call(n, nx, features, targets, ridge.reshape(1, 256))


def solution(mesh):
    n = mesh.shape["grp"]
    nx = mesh.shape["rows"] // (2 * n)
    return jax.shard_map(
        functools.partial(shards, n, nx),
        mesh=mesh,
        in_specs=(P(("rows", "grp"), None), P(("rows", "grp"), None), P()),
        out_specs=(P("rows", None), P()),
        check_vma=False,
    )
```

```python
import functools
import jax, jax.numpy as jnp
from jax import lax
from jax.experimental import pallas as pl
from jax.experimental.pallas import tpu as pltpu
from jax.sharding import PartitionSpec as P

HI = lax.Precision.HIGHEST


def mm(a, b, ca=1, cb=0):
    return lax.dot_general(a, b, (((ca,), (cb,)), ((), ())), precision=HI, preferred_element_type=jnp.float32)

def rows8(v, i):
    return jnp.broadcast_to(v[i:i+1, :], (8, 128))

def gl(v, j):
    return jnp.take_along_axis(v, jnp.full((8, 128), j, jnp.int32), axis=1)

def chol_block(a, u_ref, v_ref, base, hooks):
    lanes = lax.broadcasted_iota(jnp.int32, (8, 128), 1)
    subs = lax.broadcasted_iota(jnp.int32, (8, 128), 0)
    m = list(a)

    def spread(s):
        arow = [rows8(m[s], j) for j in range(8)]
        low = [[gl(arow[j], 8 * s + i) for j in range(i + 1)] for i in range(8)]
        return arow, low

    ahead = spread(0)
    for s in range(16):
        k = 8 * s
        if s in hooks:
            hooks[s]()
        inside = (lanes >= k) & (lanes < k + 8)
        arow, low = ahead
        near = [gl(m[s + 1], k + j) for j in range(8)] if s < 15 else None
        mixed = jnp.where(inside, jnp.where(lanes == subs + k, 1.0, 0.0), m[s])
        mrow = [rows8(mixed, j) for j in range(8)]
        bycol = [[gl(m[g], k + j) for g in range(s + 2, 16)] for j in range(8)]
        far = list(zip(*bycol))
        if s < 15:
            nxt = jnp.where(inside, 0.0, m[s + 1])
        rs = []
        for j in range(8):
            r = lax.rsqrt(low[j][j])
            rs.append(r)
            for i in range(j + 1, 8):
                low[i][j] = low[i][j] * r
            for i in range(j + 1, 8):
                for t in range(j + 1, i + 1):
                    low[i][t] = low[i][t] - low[i][j] * low[t][j]
            mrow[j] = mrow[j] * r
            for i in range(j + 1, 8):
                mrow[i] = mrow[i] - low[i][j] * mrow[j]
            if s < 15:
                near[j] = near[j] * r
                for i in range(j + 1, 8):
                    near[i] = near[i] - low[i][j] * near[j]
                nxt = nxt - near[j] * mrow[j]
        if s < 15:
            m[s + 1] = nxt
            ahead = spread(s + 1)
        if far:
            w = list(mrow)
            for j in reversed(range(8)):
                w[j] = w[j] * rs[j]
                for i in range(j):
                    w[i] = w[i] - low[j][i] * w[j]
            for g, cols in enumerate(far, start=s + 2):
                out = jnp.where(inside, 0.0, m[g])
                for j in range(8):
                    out = out - cols[j] * w[j]
                m[g] = out
        for j in range(8):
            arow[j] = arow[j] * rs[j]
            for i in range(j + 1, 8):
                arow[i] = arow[i] - low[i][j] * arow[j]
        uo, vo = arow[0], mrow[0]
        for j in range(1, 8):
            uo = jnp.where(subs == j, arow[j], uo)
            vo = jnp.where(subs == j, mrow[j], vo)
        u_ref[pl.ds(base + k, 8), pl.ds(base, 128)] = jnp.where(lanes >= subs + k, uo, 0.0)
        v_ref[pl.ds(base + k, 8), pl.ds(base, 128)] = jnp.where(lanes <= subs + k, vo, 0.0)

MESH = pl.DeviceIdType.MESH
LANES = 128


class Place:
    def __init__(self, n, nx):
        self.n, self.nx = n, nx
        rows, self.z = lax.axis_index("rows"), lax.axis_index("grp")
        self.c = rows % 2
        self.x = (rows // 2) % nx
        self.y = rows // (2 * nx)
        self.a = self.y + self.c * (self.z - self.y)
        self.b = self.z + self.c * (self.y - self.z)

    def device(self, y, x, c, z):
        return ((y * self.nx + x) * 2 + c, z)

    def partner(self):
        return self.device(self.y, self.x, 1 - self.c, self.z)

    def on_a(self, p):
        return self.device(p + self.c * (self.y - p), self.x, self.c, self.z + self.c * (p - self.z))

    def on_b(self, p):
        return self.device(self.y + self.c * (p - self.y), self.x, self.c, p + self.c * (self.z - p))

    def on_x(self, p):
        return self.device(self.y, p, self.c, self.z)

    def on_z(self, p):
        return self.device(self.y, self.x, self.c, p)


def far_first(n):
    return sorted(range(1, n), key=lambda d: -min(d, n - d))


def near_first(n):
    return sorted(range(1, n), key=lambda d: min(d, n - d))


def sum_slots(ref, count, part):
    total = ref[0, part]
    for p in range(1, count):
        total = total + ref[p, part]
    return total


def ridge_kernel(
    n, nx, f_hbm, t_hbm, ridge_ref, out_ref, fac_ref,
    feat, targ, cross, gram, gsum, csum, v_ref, q_ref,
    rc, rg, hg, g1, g2, g3, hx, bx1, sx, bx2, ha, ba1, sa, ba2, s2, b3,
    load, gpair_s, gpair_r, cpair_s, cpair_r,
    gs1, gr1, gs2, gr2, gs3, gr3, gs4, gr4, gs5, gr5,
    xs1, xr1, xs2, xr2, as1, ar1, as2, ar2, cs3, cr3, cs4, cr4,
):
    me = Place(n, nx)
    c = me.c
    gk, tz = 8 // n, 8 // n
    parts = (pl.ds(0, 1), pl.ds(1, 2))
    width = nx * 64
    sends = []

    def remote(src, dst, ssem, rsem, device):
        return pltpu.make_async_remote_copy(
            src_ref=src, dst_ref=dst, send_sem=ssem, recv_sem=rsem, device_id=device, device_id_type=MESH
        )

    def send(*what):
        copy = remote(*what)
        copy.start()
        sends.append(copy)

    def arrived(dst, rsem):
        pltpu.make_async_copy(dst, dst, rsem).wait()

    def columns(y):
        return pl.ds(pl.multiple_of(y * width, width), width)

    def load_targets(y):
        return pltpu.make_async_copy(t_hbm.at[:, columns(y)], targ.at[y], load.at[y])

    load_features = pltpu.make_async_copy(f_hbm, feat, load.at[n])
    load_features.start()
    for y in range(n):
        load_targets(y).start()

    barrier = pltpu.get_barrier_semaphore()
    greet = [me.partner()]
    greet += [me.on_a((me.a + d) % n) for d in far_first(n)]
    greet += [me.on_b((me.b + d) % n) for d in far_first(n)]
    greet += [me.on_x((me.x + d) % nx) for d in far_first(nx)]
    for device in greet:
        pl.semaphore_signal(barrier, inc=1, device_id=device, device_id_type=MESH)

    over_rows = (((0,), (0,)), ((), ()))
    load_features.wait()
    whole = lax.dot_general(feat[...], feat[...], over_rows, preferred_element_type=jnp.float32)
    gram[0] = whole[0:128, 0:128].reshape(16, 8, LANES)
    gram[1] = whole[0:128, 128:256].reshape(16, 8, LANES)
    gram[2] = whole[128:256, 128:256].reshape(16, 8, LANES)
    pl.semaphore_wait(barrier, len(greet))
    for k, part in enumerate(parts):
        send(gram.at[part, pl.ds((1 - c) * 8, 8)], rg.at[part], gpair_s.at[k], gpair_r.at[k], me.partner())

    def pair(y):
        at = pl.ds(y * nx, nx)
        return remote(cross.at[at, 1 - c], rc.at[at], cpair_s.at[y], cpair_r.at[y], me.partner())

    def turn(i):
        return (me.y + n // 2 + i) % n

    def multiply(i, carry):
        y = turn(i)
        load_targets(y).wait()
        block = lax.dot_general(targ[y], feat[...], over_rows, preferred_element_type=jnp.float32)
        cross[pl.ds(y * nx, nx)] = block.reshape(nx, 2, 32, 256)
        pair(y).start()
        return carry

    def pass_on(i):
        y = turn(i)
        arrived(rc.at[pl.ds(y * nx, nx)], cpair_r.at[y])
        for x in range(nx):
            blk = y * nx + x
            for q in range(8):
                rt, lh = q // 2, q % 2
                z, t = q // tz, q % tz
                upper = (pl.ds(8 * rt, 4), pl.ds(LANES * lh, LANES))
                lower = (pl.ds(8 * rt + 4, 4), pl.ds(LANES * lh, LANES))
                hx[x, y, z, t] = cross[(blk, c) + upper] + rc[(blk,) + upper]
                ha[y + c * (z - y), z + c * (y - z), x, t] = cross[(blk, c) + lower] + rc[(blk,) + lower]
        for d in far_first(nx):
            p = (me.x + d) % nx
            remote(hx.at[p, y], bx1.at[me.x, y], xs1.at[p], xr1.at[me.x], me.on_x(p)).start()

        @pl.when((c == 0) & (y != me.y))
        def _():
            remote(ha.at[y], ba1.at[me.a], as1.at[y], ar1.at[me.a], me.on_a(y)).start()

        @pl.when(c == 1)
        def _():
            for d in far_first(n):
                p = (me.a + d) % n
                remote(ha.at[p, y], ba1.at[me.a, y], as1.at[p], ar1.at[me.a], me.on_a(p)).start()

    def both(i, carry):
        multiply(i, carry)
        pass_on(i - n // 2)
        return carry

    def rest(i, carry):
        pass_on(i)
        return carry

    lax.fori_loop(0, n // 2, multiply, 0)
    for k, part in enumerate(parts):
        arrived(rg.at[part], gpair_r.at[k])
        for p in range(n):
            hg[p, part] = gram[part, pl.ds(c * 8 + p * gk, gk)] + rg[part, pl.ds(p * gk, gk)]
        for d in far_first(n):
            p = (me.a + d) % n
            send(hg.at[p, part], g1.at[me.a, part], gs1.at[k * n + d], gr1.at[k * n + me.a], me.on_a(p))
        g1[me.a, part] = hg[me.a, part]
    lax.fori_loop(n // 2, n, both, 0)
    lax.fori_loop(n // 2, n, rest, 0)

    def sum_first():
        for d in near_first(nx):
            p = (me.x + d) % nx
            arrived(bx1.at[p], xr1.at[p])

        def add_x(p, carry):
            for r in range(n):
                y, z = p + c * (r - p), r + c * (p - r)
                total = hx[me.x, y, z]
                for d in range(1, nx):
                    total = total + bx1[(me.x + d) % nx, y, z]
                sx[p, r] = total
            return carry

        lax.fori_loop(0, n, add_x, 0)
        for d in far_first(n):
            p = (me.a + d) % n
            send(sx.at[p], bx2.at[me.a], xs2.at[d], xr2.at[me.a], me.on_a(p))
        for d in near_first(n):
            p = (me.a + d) % n
            arrived(ba1.at[p], ar1.at[p])

        def add_a(r, carry):
            for x in range(nx):
                total = ha[me.a, r, x]
                for d in range(1, n):
                    total = total + ba1[(me.a + d) % n, r, x]
                sa[x, r] = total
            return carry

        lax.fori_loop(0, n, add_a, 0)
        for d in far_first(nx):
            p = (me.x + d) % nx
            send(sa.at[p], ba2.at[me.x], as2.at[d], ar2.at[me.x], me.on_x(p))

    def sum_second():
        total = sa[me.x]
        for d in near_first(nx):
            p = (me.x + d) % nx
            arrived(ba2.at[p], ar2.at[p])
            total = total + ba2[p]
        s2[:, :, 4:8, :] = total
        total = sx[me.a]
        for d in near_first(n):
            p = (me.a + d) % n
            arrived(bx2.at[p], xr2.at[p])
            total = total + bx2[p]
        s2[:, :, 0:4, :] = total
        for d in far_first(n):
            p = (me.b + d) % n
            send(s2.at[p], b3.at[me.b], cs3.at[d], cr3.at[me.b], me.on_b(p))

    mine = pl.ds(me.z * tz, tz)

    def sum_third():
        total = s2[me.b]
        for d in near_first(n):
            p = (me.b + d) % n
            arrived(b3.at[p], cr3.at[p])
            total = total + b3[p]
        csum[mine] = total
        for d in far_first(n):
            send(csum.at[mine], csum.at[mine], cs4.at[d], cr4.at[me.z], me.on_z((me.z + d) % n))

    def over_x(k):
        part = parts[k]
        for d in near_first(n):
            p = (me.a + d) % n
            arrived(g1.at[p, part], gr1.at[k * n + p])
        g2[me.x, part] = sum_slots(g1, n, part)
        mine = g2.at[me.x, part]
        for d in far_first(nx):
            send(mine, mine, gs2.at[k * nx + d], gr2.at[k * nx + me.x], me.on_x((me.x + d) % nx))

    def over_b(k):
        part = parts[k]
        for d in near_first(nx):
            p = (me.x + d) % nx
            arrived(g2.at[p, part], gr2.at[k * nx + p])
        g3[me.b, part] = sum_slots(g2, nx, part)
        mine = g3.at[me.b, part]
        for d in far_first(n):
            send(mine, mine, gs3.at[k * n + d], gr3.at[k * n + me.b], me.on_b((me.b + d) % n))

    def owned(k, core, p):
        return gsum.at[parts[k], pl.ds(core * 8 + p * gk, gk)]

    def gather(k):
        part = parts[k]
        for d in near_first(n):
            p = (me.b + d) % n
            arrived(g3.at[p, part], gr3.at[k * n + p])
        mine = owned(k, c, me.a)
        mine[...] = sum_slots(g3, n, part)
        for d in far_first(n):
            send(mine, mine, gs4.at[k * n + d], gr4.at[k * n + me.a], me.on_a((me.a + d) % n))
        send(mine, mine, gs5.at[k * n + me.a], gr5.at[k * n + me.a], me.partner())

    def forward(k):
        for d in near_first(n):
            p = (me.a + d) % n
            block = owned(k, c, p)
            arrived(block, gr4.at[k * n + p])
            send(block, block, gs5.at[k * n + p], gr5.at[k * n + p], me.partner())

    def complete(k):
        for p in range(n):
            arrived(owned(k, 1 - c, p), gr5.at[k * n + p])

    over_x(0)
    over_x(1)
    over_b(0)
    over_b(1)
    sum_first()
    gather(0)
    gather(1)
    sum_second()
    forward(0)
    complete(0)
    lanes = lax.broadcasted_iota(jnp.int32, (8, 128), 1)
    subs = lax.broadcasted_iota(jnp.int32, (8, 128), 0)

    def ridged(tile, g, start):
        values = jnp.broadcast_to(ridge_ref[0:1, start:start + 128], (8, 128))
        return tile + jnp.where(lanes == subs + 8 * g, values, 0.0)

    chol_block([ridged(gsum[0, g], g, 0) for g in range(16)], fac_ref, v_ref, 0, {1: lambda: forward(1), 2: sum_third})
    complete(1)
    v11 = v_ref[0:128, 0:128]
    u12 = mm(v11, gsum[1].reshape(128, 128))
    fac_ref[0:128, 128:256] = u12
    fac_ref[128:256, 0:128] = jnp.zeros((128, 128), jnp.float32)
    v_ref[0:128, 128:256] = jnp.zeros((128, 128), jnp.float32)
    q_ref[0] = mm(u12, u12, 0, 0)
    q_ref[1] = mm(u12, v11, 0, 0)
    trailing = [ridged(gsum[2, g], g, 128) - q_ref[0, pl.ds(8 * g, 8), :] for g in range(16)]
    chol_block(trailing, fac_ref, v_ref, 128, {})
    v_ref[128:256, 0:128] = -mm(v_ref[128:256, 128:256], q_ref[1])

    for d in near_first(n):
        p = (me.z + d) % n
        arrived(csum.at[pl.ds(p * tz, tz)], cr4.at[p])
    left = jnp.concatenate([csum[2 * t] for t in range(4)], axis=0)
    right = jnp.concatenate([csum[2 * t + 1] for t in range(4)], axis=0)
    halfway = mm(jnp.concatenate([left, right], axis=1), v_ref[...], 1, 1)
    out_ref[...] = mm(halfway, v_ref[...])

    def sent(y, carry):
        pair(y).wait_send()
        return carry

    lax.fori_loop(0, n, sent, 0)
    for d in range(1, nx):
        p = (me.x + d) % nx
        remote(hx.at[p], bx1.at[me.x], xs1.at[p], xr1.at[me.x], me.on_x(p)).wait_send()
    for d in range(1, n):
        p = (me.a + d) % n
        remote(ha.at[p], ba1.at[me.a], as1.at[p], ar1.at[me.a], me.on_a(p)).wait_send()
    for copy in sends:
        copy.wait_send()


def ridge_call(n, nx, features, targets, ridge):
    gk, tz = 8 // n, 8 // n
    rows = features.shape[0]
    f32 = lambda *shape: pltpu.VMEM(shape, jnp.float32)
    tiles = lambda *lead: f32(*lead, 8, LANES)
    halves = lambda *lead: f32(*lead, 4, LANES)
    dma = lambda k: pltpu.SemaphoreType.DMA((k,))
    vmem, hbm = pl.BlockSpec(memory_space=pltpu.VMEM), pl.BlockSpec(memory_space=pltpu.HBM)
    return pl.pallas_call(
        functools.partial(ridge_kernel, n, nx),
        out_shape=(
            jax.ShapeDtypeStruct((32, 256), jnp.float32),
            jax.ShapeDtypeStruct((256, 256), jnp.float32),
        ),
        in_specs=[hbm, hbm, vmem],
        out_specs=(vmem, vmem),
        scratch_shapes=[
            pltpu.VMEM((rows, 256), jnp.bfloat16), pltpu.VMEM((n, rows, nx * 64), jnp.bfloat16),
            f32(n * nx, 2, 32, 256), tiles(3, 16), tiles(3, 16), tiles(8), f32(256, 256), f32(2, 128, 128),
            f32(n * nx, 32, 256), tiles(3, 8), tiles(n, 3, gk), tiles(n, 3, gk), tiles(nx, 3, gk), tiles(n, 3, gk),
            halves(nx, n, n, tz), halves(nx, n, n, tz), halves(n, n, tz), halves(n, n, tz),
            halves(n, n, nx, tz), halves(n, n, nx, tz), halves(nx, n, tz), halves(nx, n, tz), tiles(n, tz), tiles(n, tz),
            dma(n + 1), dma(2), dma(2), dma(n), dma(n),
            dma(2 * n), dma(2 * n), dma(2 * nx), dma(2 * nx), dma(2 * n), dma(2 * n), dma(2 * n), dma(2 * n), dma(2 * n), dma(2 * n),
            dma(nx), dma(nx), dma(n), dma(n), dma(n), dma(n), dma(nx), dma(nx), dma(n), dma(n), dma(n), dma(n),
        ],
        compiler_params=pltpu.CompilerParams(collective_id=0, has_side_effects=True),
    )(features, targets, ridge)


def hand_kernel(read_in, fac_in, read_out, fac_out, read_v, fac_v, came, went):
    chunk = 64
    takes = [pltpu.make_async_copy(read_in, read_v, came.at[4])]
    gives = [pltpu.make_async_copy(read_v, read_out, went.at[4])]
    for k in range(4):
        rows = pl.ds(chunk * k, chunk)
        takes.append(pltpu.make_async_copy(fac_in.at[rows], fac_v.at[rows], came.at[k]))
        gives.append(pltpu.make_async_copy(fac_v.at[rows], fac_out.at[rows], went.at[k]))
    for take in takes:
        take.start()
    for take, give in zip(takes, gives):
        take.wait()
        give.start()
    for give in gives:
        give.wait()


def hand_call(readout, factor):
    hbm = pl.BlockSpec(memory_space=pltpu.HBM)
    return pl.pallas_call(
        hand_kernel,
        out_shape=(jax.ShapeDtypeStruct((32, 256), jnp.float32), jax.ShapeDtypeStruct((256, 256), jnp.float32)),
        in_specs=[hbm, hbm],
        out_specs=(hbm, hbm),
        scratch_shapes=[
            pltpu.VMEM((32, 256), jnp.float32), pltpu.VMEM((256, 256), jnp.float32),
            pltpu.SemaphoreType.DMA((5,)), pltpu.SemaphoreType.DMA((5,)),
        ],
    )(readout, factor)


def shards(n, nx, features, targets, ridge):
    return hand_call(*ridge_call(n, nx, features, targets, ridge.reshape(1, 256)))


def solution(mesh):
    n = mesh.shape["grp"]
    nx = mesh.shape["rows"] // (2 * n)
    return jax.shard_map(
        functools.partial(shards, n, nx),
        mesh=mesh,
        in_specs=(P(("rows", "grp"), None), P(("rows", "grp"), None), P()),
        out_specs=(P("rows", None), P()),
        check_vma=False,
    )
```

```python
import functools
import jax, jax.numpy as jnp
from jax import lax
from jax.experimental import pallas as pl
from jax.experimental.pallas import tpu as pltpu
from jax.sharding import PartitionSpec as P

HI = lax.Precision.HIGHEST


def mm(a, b, ca=1, cb=0):
    return lax.dot_general(a, b, (((ca,), (cb,)), ((), ())), precision=HI, preferred_element_type=jnp.float32)

def rows8(v, i):
    return jnp.broadcast_to(v[i:i+1, :], (8, 128))

def gl(v, j):
    return jnp.take_along_axis(v, jnp.full((8, 128), j, jnp.int32), axis=1)

def chol_block(a, u_ref, v_ref, base, hooks):
    lanes = lax.broadcasted_iota(jnp.int32, (8, 128), 1)
    subs = lax.broadcasted_iota(jnp.int32, (8, 128), 0)
    m = list(a)

    def spread(s):
        arow = [rows8(m[s], j) for j in range(8)]
        low = [[gl(arow[j], 8 * s + i) for j in range(i + 1)] for i in range(8)]
        return arow, low

    ahead = spread(0)
    for s in range(16):
        k = 8 * s
        if s in hooks:
            hooks[s]()
        inside = (lanes >= k) & (lanes < k + 8)
        arow, low = ahead
        near = [gl(m[s + 1], k + j) for j in range(8)] if s < 15 else None
        mixed = jnp.where(inside, jnp.where(lanes == subs + k, 1.0, 0.0), m[s])
        mrow = [rows8(mixed, j) for j in range(8)]
        bycol = [[gl(m[g], k + j) for g in range(s + 2, 16)] for j in range(8)]
        far = list(zip(*bycol))
        if s < 15:
            nxt = jnp.where(inside, 0.0, m[s + 1])
        rs = []
        for j in range(8):
            r = lax.rsqrt(low[j][j])
            rs.append(r)
            for i in range(j + 1, 8):
                low[i][j] = low[i][j] * r
            for i in range(j + 1, 8):
                for t in range(j + 1, i + 1):
                    low[i][t] = low[i][t] - low[i][j] * low[t][j]
            mrow[j] = mrow[j] * r
            for i in range(j + 1, 8):
                mrow[i] = mrow[i] - low[i][j] * mrow[j]
            if s < 15:
                near[j] = near[j] * r
                for i in range(j + 1, 8):
                    near[i] = near[i] - low[i][j] * near[j]
                nxt = nxt - near[j] * mrow[j]
        if s < 15:
            m[s + 1] = nxt
            ahead = spread(s + 1)
        if far:
            w = list(mrow)
            for j in reversed(range(8)):
                w[j] = w[j] * rs[j]
                for i in range(j):
                    w[i] = w[i] - low[j][i] * w[j]
            for g, cols in enumerate(far, start=s + 2):
                out = jnp.where(inside, 0.0, m[g])
                for j in range(8):
                    out = out - cols[j] * w[j]
                m[g] = out
        for j in range(8):
            arow[j] = arow[j] * rs[j]
            for i in range(j + 1, 8):
                arow[i] = arow[i] - low[i][j] * arow[j]
        uo, vo = arow[0], mrow[0]
        for j in range(1, 8):
            uo = jnp.where(subs == j, arow[j], uo)
            vo = jnp.where(subs == j, mrow[j], vo)
        u_ref[pl.ds(base + k, 8), pl.ds(base, 128)] = jnp.where(lanes >= subs + k, uo, 0.0)
        v_ref[pl.ds(base + k, 8), pl.ds(base, 128)] = jnp.where(lanes <= subs + k, vo, 0.0)

MESH = pl.DeviceIdType.MESH
LANES = 128


class Place:
    def __init__(self, n, nx):
        self.n, self.nx = n, nx
        rows, self.z = lax.axis_index("rows"), lax.axis_index("grp")
        self.c = rows % 2
        self.x = (rows // 2) % nx
        self.y = rows // (2 * nx)
        self.a = self.y + self.c * (self.z - self.y)
        self.b = self.z + self.c * (self.y - self.z)

    def device(self, y, x, c, z):
        return ((y * self.nx + x) * 2 + c, z)

    def partner(self):
        return self.device(self.y, self.x, 1 - self.c, self.z)

    def on_a(self, p):
        return self.device(p + self.c * (self.y - p), self.x, self.c, self.z + self.c * (p - self.z))

    def on_b(self, p):
        return self.device(self.y + self.c * (p - self.y), self.x, self.c, p + self.c * (self.z - p))

    def on_x(self, p):
        return self.device(self.y, p, self.c, self.z)

    def on_z(self, p):
        return self.device(self.y, self.x, self.c, p)


def far_first(n):
    return sorted(range(1, n), key=lambda d: -min(d, n - d))


def near_first(n):
    return sorted(range(1, n), key=lambda d: min(d, n - d))


def sum_slots(ref, count, part):
    total = ref[0, part]
    for p in range(1, count):
        total = total + ref[p, part]
    return total


def ridge_kernel(
    n, nx, f_hbm, t_hbm, ridge_ref, out_ref, fac_ref,
    feat, targ, cross, gram, gsum, csum, v_ref, q_ref,
    rc, rg, hg, g1, g2, g3, hx, bx1, sx, bx2, ha, ba1, sa, ba2, s2, b3,
    load, gpair_s, gpair_r, cpair_s, cpair_r,
    gs1, gr1, gs2, gr2, gs3, gr3, gs4, gr4, gs5, gr5,
    xs1, xr1, xs2, xr2, as1, ar1, as2, ar2, cs3, cr3, cs4, cr4,
):
    me = Place(n, nx)
    c = me.c
    gk, tz = 8 // n, 8 // n
    parts = (pl.ds(0, 1), pl.ds(1, 2))
    width = nx * 64
    sends = []

    def remote(src, dst, ssem, rsem, device):
        return pltpu.make_async_remote_copy(
            src_ref=src, dst_ref=dst, send_sem=ssem, recv_sem=rsem, device_id=device, device_id_type=MESH
        )

    def send(*what):
        copy = remote(*what)
        copy.start()
        sends.append(copy)

    def arrived(dst, rsem):
        pltpu.make_async_copy(dst, dst, rsem).wait()

    def columns(y):
        return pl.ds(pl.multiple_of(y * width, width), width)

    def load_targets(y):
        return pltpu.make_async_copy(t_hbm.at[:, columns(y)], targ.at[y], load.at[y])

    load_features = pltpu.make_async_copy(f_hbm, feat, load.at[n])
    load_features.start()
    for y in range(n):
        load_targets(y).start()

    barrier = pltpu.get_barrier_semaphore()
    greet = [me.partner()]
    greet += [me.on_a((me.a + d) % n) for d in far_first(n)]
    greet += [me.on_b((me.b + d) % n) for d in far_first(n)]
    greet += [me.on_x((me.x + d) % nx) for d in far_first(nx)]
    for device in greet:
        pl.semaphore_signal(barrier, inc=1, device_id=device, device_id_type=MESH)

    over_rows = (((0,), (0,)), ((), ()))
    load_features.wait()
    whole = lax.dot_general(feat[...], feat[...], over_rows, preferred_element_type=jnp.float32)
    gram[0] = whole[0:128, 0:128].reshape(16, 8, LANES)
    gram[1] = whole[0:128, 128:256].reshape(16, 8, LANES)
    gram[2] = whole[128:256, 128:256].reshape(16, 8, LANES)
    pl.semaphore_wait(barrier, len(greet))
    for k, part in enumerate(parts):
        send(gram.at[part, pl.ds((1 - c) * 8, 8)], rg.at[part], gpair_s.at[k], gpair_r.at[k], me.partner())

    def pair(y):
        at = pl.ds(y * nx, nx)
        return remote(cross.at[at, 1 - c], rc.at[at], cpair_s.at[y], cpair_r.at[y], me.partner())

    def turn(i):
        return (me.y + n // 2 + i) % n

    def multiply(i, carry):
        y = turn(i)
        load_targets(y).wait()
        block = lax.dot_general(targ[y], feat[...], over_rows, preferred_element_type=jnp.float32)
        cross[pl.ds(y * nx, nx)] = block.reshape(nx, 2, 32, 256)
        pair(y).start()
        return carry

    def pass_on(i):
        y = turn(i)
        arrived(rc.at[pl.ds(y * nx, nx)], cpair_r.at[y])
        for x in range(nx):
            blk = y * nx + x
            for q in range(8):
                rt, lh = q // 2, q % 2
                z, t = q // tz, q % tz
                upper = (pl.ds(8 * rt, 4), pl.ds(LANES * lh, LANES))
                lower = (pl.ds(8 * rt + 4, 4), pl.ds(LANES * lh, LANES))
                hx[x, y, z, t] = cross[(blk, c) + upper] + rc[(blk,) + upper]
                ha[y + c * (z - y), z + c * (y - z), x, t] = cross[(blk, c) + lower] + rc[(blk,) + lower]
        for d in far_first(nx):
            p = (me.x + d) % nx
            remote(hx.at[p, y], bx1.at[me.x, y], xs1.at[p], xr1.at[me.x], me.on_x(p)).start()

        @pl.when((c == 0) & (y != me.y))
        def _():
            remote(ha.at[y], ba1.at[me.a], as1.at[y], ar1.at[me.a], me.on_a(y)).start()

        @pl.when(c == 1)
        def _():
            for d in far_first(n):
                p = (me.a + d) % n
                remote(ha.at[p, y], ba1.at[me.a, y], as1.at[p], ar1.at[me.a], me.on_a(p)).start()

    def both(i, carry):
        multiply(i, carry)
        pass_on(i - n // 2)
        return carry

    def rest(i, carry):
        pass_on(i)
        return carry

    lax.fori_loop(0, n // 2, multiply, 0)
    for k, part in enumerate(parts):
        arrived(rg.at[part], gpair_r.at[k])
        for p in range(n):
            hg[p, part] = gram[part, pl.ds(c * 8 + p * gk, gk)] + rg[part, pl.ds(p * gk, gk)]
        for d in far_first(n):
            p = (me.a + d) % n
            send(hg.at[p, part], g1.at[me.a, part], gs1.at[k * n + d], gr1.at[k * n + me.a], me.on_a(p))
        g1[me.a, part] = hg[me.a, part]
    lax.fori_loop(n // 2, n, both, 0)
    lax.fori_loop(n // 2, n, rest, 0)

    def sum_first():
        for d in near_first(nx):
            p = (me.x + d) % nx
            arrived(bx1.at[p], xr1.at[p])

        def add_x(p, carry):
            for r in range(n):
                y, z = p + c * (r - p), r + c * (p - r)
                total = hx[me.x, y, z]
                for d in range(1, nx):
                    total = total + bx1[(me.x + d) % nx, y, z]
                sx[p, r] = total
            return carry

        lax.fori_loop(0, n, add_x, 0)
        for d in far_first(n):
            p = (me.a + d) % n
            send(sx.at[p], bx2.at[me.a], xs2.at[d], xr2.at[me.a], me.on_a(p))
        for d in near_first(n):
            p = (me.a + d) % n
            arrived(ba1.at[p], ar1.at[p])

        def add_a(r, carry):
            for x in range(nx):
                total = ha[me.a, r, x]
                for d in range(1, n):
                    total = total + ba1[(me.a + d) % n, r, x]
                sa[x, r] = total
            return carry

        lax.fori_loop(0, n, add_a, 0)
        for d in far_first(nx):
            p = (me.x + d) % nx
            send(sa.at[p], ba2.at[me.x], as2.at[d], ar2.at[me.x], me.on_x(p))

    def sum_second():
        total = sa[me.x]
        for d in near_first(nx):
            p = (me.x + d) % nx
            arrived(ba2.at[p], ar2.at[p])
            total = total + ba2[p]
        s2[:, :, 4:8, :] = total
        total = sx[me.a]
        for d in near_first(n):
            p = (me.a + d) % n
            arrived(bx2.at[p], xr2.at[p])
            total = total + bx2[p]
        s2[:, :, 0:4, :] = total
        for d in far_first(n):
            p = (me.b + d) % n
            send(s2.at[p], b3.at[me.b], cs3.at[d], cr3.at[me.b], me.on_b(p))

    mine = pl.ds(me.z * tz, tz)

    def sum_third():
        total = s2[me.b]
        for d in near_first(n):
            p = (me.b + d) % n
            arrived(b3.at[p], cr3.at[p])
            total = total + b3[p]
        csum[mine] = total
        for d in far_first(n):
            send(csum.at[mine], csum.at[mine], cs4.at[d], cr4.at[me.z], me.on_z((me.z + d) % n))

    def over_x(k):
        part = parts[k]
        for d in near_first(n):
            p = (me.a + d) % n
            arrived(g1.at[p, part], gr1.at[k * n + p])
        g2[me.x, part] = sum_slots(g1, n, part)
        mine = g2.at[me.x, part]
        for d in far_first(nx):
            send(mine, mine, gs2.at[k * nx + d], gr2.at[k * nx + me.x], me.on_x((me.x + d) % nx))

    def over_b(k):
        part = parts[k]
        for d in near_first(nx):
            p = (me.x + d) % nx
            arrived(g2.at[p, part], gr2.at[k * nx + p])
        g3[me.b, part] = sum_slots(g2, nx, part)
        mine = g3.at[me.b, part]
        for d in far_first(n):
            send(mine, mine, gs3.at[k * n + d], gr3.at[k * n + me.b], me.on_b((me.b + d) % n))

    def owned(k, core, p):
        return gsum.at[parts[k], pl.ds(core * 8 + p * gk, gk)]

    def gather(k):
        part = parts[k]
        for d in near_first(n):
            p = (me.b + d) % n
            arrived(g3.at[p, part], gr3.at[k * n + p])
        mine = owned(k, c, me.a)
        mine[...] = sum_slots(g3, n, part)
        for d in far_first(n):
            send(mine, mine, gs4.at[k * n + d], gr4.at[k * n + me.a], me.on_a((me.a + d) % n))
        send(mine, mine, gs5.at[k * n + me.a], gr5.at[k * n + me.a], me.partner())

    def forward(k):
        for d in near_first(n):
            p = (me.a + d) % n
            block = owned(k, c, p)
            arrived(block, gr4.at[k * n + p])
            send(block, block, gs5.at[k * n + p], gr5.at[k * n + p], me.partner())

    def complete(k):
        for p in range(n):
            arrived(owned(k, 1 - c, p), gr5.at[k * n + p])

    over_x(0)
    over_x(1)
    over_b(0)
    over_b(1)
    sum_first()
    gather(0)
    gather(1)
    sum_second()
    forward(0)
    complete(0)
    lanes = lax.broadcasted_iota(jnp.int32, (8, 128), 1)
    subs = lax.broadcasted_iota(jnp.int32, (8, 128), 0)

    def ridged(tile, g, start):
        values = jnp.broadcast_to(ridge_ref[0:1, start:start + 128], (8, 128))
        return tile + jnp.where(lanes == subs + 8 * g, values, 0.0)

    chol_block([ridged(gsum[0, g], g, 0) for g in range(16)], fac_ref, v_ref, 0, {1: lambda: forward(1), 2: sum_third})
    complete(1)
    v11 = v_ref[0:128, 0:128]
    u12 = mm(v11, gsum[1].reshape(128, 128))
    fac_ref[0:128, 128:256] = u12
    fac_ref[128:256, 0:128] = jnp.zeros((128, 128), jnp.float32)
    v_ref[0:128, 128:256] = jnp.zeros((128, 128), jnp.float32)
    square = mm(u12, u12, 0, 0)

    def corner():
        q_ref[...] = mm(u12, v11, 0, 0)

    trailing = [ridged(gsum[2, g], g, 128) - square[8 * g:8 * g + 8, :] for g in range(16)]
    chol_block(trailing, fac_ref, v_ref, 128, {4: corner})
    v_ref[128:256, 0:128] = -mm(v_ref[128:256, 128:256], q_ref[...])

    for d in near_first(n):
        p = (me.z + d) % n
        arrived(csum.at[pl.ds(p * tz, tz)], cr4.at[p])
    left = jnp.concatenate([csum[2 * t] for t in range(4)], axis=0)
    right = jnp.concatenate([csum[2 * t + 1] for t in range(4)], axis=0)
    halfway = mm(jnp.concatenate([left, right], axis=1), v_ref[...], 1, 1)
    out_ref[...] = mm(halfway, v_ref[...])

    def sent(y, carry):
        pair(y).wait_send()
        return carry

    lax.fori_loop(0, n, sent, 0)
    for d in range(1, nx):
        p = (me.x + d) % nx
        remote(hx.at[p], bx1.at[me.x], xs1.at[p], xr1.at[me.x], me.on_x(p)).wait_send()
    for d in range(1, n):
        p = (me.a + d) % n
        remote(ha.at[p], ba1.at[me.a], as1.at[p], ar1.at[me.a], me.on_a(p)).wait_send()
    for copy in sends:
        copy.wait_send()


def ridge_call(n, nx, features, targets, ridge):
    gk, tz = 8 // n, 8 // n
    rows = features.shape[0]
    f32 = lambda *shape: pltpu.VMEM(shape, jnp.float32)
    tiles = lambda *lead: f32(*lead, 8, LANES)
    halves = lambda *lead: f32(*lead, 4, LANES)
    dma = lambda k: pltpu.SemaphoreType.DMA((k,))
    vmem, hbm = pl.BlockSpec(memory_space=pltpu.VMEM), pl.BlockSpec(memory_space=pltpu.HBM)
    return pl.pallas_call(
        functools.partial(ridge_kernel, n, nx),
        out_shape=(
            jax.ShapeDtypeStruct((32, 256), jnp.float32),
            jax.ShapeDtypeStruct((256, 256), jnp.float32),
        ),
        in_specs=[hbm, hbm, vmem],
        out_specs=(vmem, vmem),
        scratch_shapes=[
            pltpu.VMEM((rows, 256), jnp.bfloat16), pltpu.VMEM((n, rows, nx * 64), jnp.bfloat16),
            f32(n * nx, 2, 32, 256), tiles(3, 16), tiles(3, 16), tiles(8), f32(256, 256), f32(128, 128),
            f32(n * nx, 32, 256), tiles(3, 8), tiles(n, 3, gk), tiles(n, 3, gk), tiles(nx, 3, gk), tiles(n, 3, gk),
            halves(nx, n, n, tz), halves(nx, n, n, tz), halves(n, n, tz), halves(n, n, tz),
            halves(n, n, nx, tz), halves(n, n, nx, tz), halves(nx, n, tz), halves(nx, n, tz), tiles(n, tz), tiles(n, tz),
            dma(n + 1), dma(2), dma(2), dma(n), dma(n),
            dma(2 * n), dma(2 * n), dma(2 * nx), dma(2 * nx), dma(2 * n), dma(2 * n), dma(2 * n), dma(2 * n), dma(2 * n), dma(2 * n),
            dma(nx), dma(nx), dma(n), dma(n), dma(n), dma(n), dma(nx), dma(nx), dma(n), dma(n), dma(n), dma(n),
        ],
        compiler_params=pltpu.CompilerParams(collective_id=0, has_side_effects=True),
    )(features, targets, ridge)


def hand_kernel(read_in, fac_in, read_out, fac_out, read_v, fac_v, came, went):
    chunk = 64
    takes = [pltpu.make_async_copy(read_in, read_v, came.at[4])]
    gives = [pltpu.make_async_copy(read_v, read_out, went.at[4])]
    for k in range(4):
        rows = pl.ds(chunk * k, chunk)
        takes.append(pltpu.make_async_copy(fac_in.at[rows], fac_v.at[rows], came.at[k]))
        gives.append(pltpu.make_async_copy(fac_v.at[rows], fac_out.at[rows], went.at[k]))
    for take in takes:
        take.start()
    for take, give in zip(takes, gives):
        take.wait()
        give.start()
    for give in gives:
        give.wait()


def hand_call(readout, factor):
    hbm = pl.BlockSpec(memory_space=pltpu.HBM)
    return pl.pallas_call(
        hand_kernel,
        out_shape=(jax.ShapeDtypeStruct((32, 256), jnp.float32), jax.ShapeDtypeStruct((256, 256), jnp.float32)),
        in_specs=[hbm, hbm],
        out_specs=(hbm, hbm),
        scratch_shapes=[
            pltpu.VMEM((32, 256), jnp.float32), pltpu.VMEM((256, 256), jnp.float32),
            pltpu.SemaphoreType.DMA((5,)), pltpu.SemaphoreType.DMA((5,)),
        ],
    )(readout, factor)


def shards(n, nx, features, targets, ridge):
    return hand_call(*ridge_call(n, nx, features, targets, ridge.reshape(1, 256)))


def solution(mesh):
    n = mesh.shape["grp"]
    nx = mesh.shape["rows"] // (2 * n)
    return jax.shard_map(
        functools.partial(shards, n, nx),
        mesh=mesh,
        in_specs=(P(("rows", "grp"), None), P(("rows", "grp"), None), P()),
        out_specs=(P("rows", None), P()),
        check_vma=False,
    )
```
